32 devices in a mesh: row: 8 (over y, x, core), col: 4 (over z).
Axes of the slice: x: 2, y: 2, z: 4, core: 2. Of those that a mesh axis runs over, the one named last changes fastest.
Arguments:
- front_rows: bfloat16 [32, 128, 512], P('row', 'col'), may hold values from -0.109375 to 0.109375
- slot_blocks: int32 [32], P('row'), may hold values from -1 to 23, as said below
- inv_factor: float32 [512, 512], replicated
- ancestor_inv: float32 [3072, 3072], P('row', 'col'), may hold values from -6 to 6
Outputs:
- offdiag_inv: float32 [3072, 512], P(('row', 'col'))
- diag_inv: float32 [512, 512], P('col')
The draws below stay inside these ranges and needn't reach their ends.
Inputs may be any that keep to these rules, and one draw needn't show every extreme that they name: `slot_blocks`: each of the 24 blocks stands in exactly one slot and -1 marks an empty slot. Block b belongs to column panel b // 6; the 4 slots of one row index hold at most 1 block of one panel, and some row index holds exactly 1 block of every panel.
All inputs are finite; a program needn't handle non-finite values.
Results may differ from the reference program's by a relative error of at most 0.0041.
Values may be sent and summed in bfloat16 or wider, within the bound.
A program may use at most 64 MiB of HBM per device.

```python
import math
import jax
import jax.numpy as jnp
from jax import lax

W = 512
BLK = 128
TILE_ROWS = 384
M = 3072
PANEL_ROWS = 768
PANEL_BLOCKS = 6
CAND = 1
SLOTS = 4
N_ROW = 8
N_COL = 4


def draw_slot_blocks(key, part):
    row_count = M // TILE_ROWS
    col_count = SLOTS // CAND
    subkeys = jax.random.split(key, 5)
    full_row = jax.random.randint(subkeys[0], (), 0, row_count)
    weight = jax.random.randint(subkeys[1], (row_count,), 0, 8)
    spot_count = row_count * CAND
    spot_row = jnp.arange(spot_count) // CAND
    raw_scores = jax.random.randint(subkeys[2], (col_count, spot_count), 0, 4096)
    scores = raw_scores // (1 + weight[spot_row])[None, :] * spot_count + jnp.arange(spot_count)[None, :]
    scores = jnp.where(spot_row[None, :] == full_row, 4096 * spot_count + spot_count, scores)
    ranked = jnp.argsort(scores, axis=1)
    remaining = PANEL_BLOCKS - CAND
    chosen = ranked[:, :remaining]
    shuffle = jnp.argsort(jax.random.randint(subkeys[3], (col_count, PANEL_BLOCKS), 0, 65536) * PANEL_BLOCKS + jnp.arange(PANEL_BLOCKS)[None, :], axis=1)
    block_ids = (shuffle + (jnp.arange(col_count) * PANEL_BLOCKS)[:, None]).astype(jnp.int32)
    full_spots = full_row * CAND + jnp.arange(CAND)
    panel_iota = jnp.arange(col_count)[:, None]
    slot_table = jnp.full((col_count, spot_count), -1, jnp.int32)
    slot_table = slot_table.at[panel_iota, full_spots[None, :]].set(block_ids[:, :CAND])
    slot_table = slot_table.at[panel_iota, chosen].set(block_ids[:, CAND:])
    slot_table = slot_table.reshape(col_count, row_count, CAND).transpose(1, 0, 2).reshape(row_count, SLOTS)
    mixing = jax.random.randint(subkeys[4], (row_count, SLOTS), 0, 65536) * SLOTS + jnp.arange(SLOTS)[None, :]
    shuffle_rows = jnp.argsort(mixing, axis=1)
    slot_table = jnp.take_along_axis(slot_table, shuffle_rows, axis=1)
    return slot_table.reshape(-1).astype(jnp.int32)


def draw_inv_factor(key, part):
    first_key, second_key = jax.random.split(key)
    lower_part = jax.random.normal(first_key, (W, W), jnp.float32) / math.sqrt(W)
    diagonal_part = jax.random.uniform(second_key, (W,), jnp.float32, 1.0, 2.0)
    return jnp.tril(lower_part, -1) + jnp.diag(diagonal_part)


def spiked(values, own_key, source, target, blocks, factor):
    owner, partner = [(jnp.arange(values.shape[position]) // (values.shape[position] // blocks)).reshape([-1 if axis == position else 1 for axis in range(values.ndim)]) for position in (source, target)]
    chosen = jax.random.permutation(own_key, blocks)[partner]
    strong = (owner == chosen) | (owner == (partner + blocks // 2) % blocks)
    return jnp.where(strong, factor * values, values)


def steps_of(own_key, extent, shards, least, top_value):
    loudness, own = 1.0, jax.random.fold_in(own_key, 6)
    for dim, parts in shards:
        draws = jnp.exp(jax.random.uniform(jax.random.fold_in(own, dim), (parts,), jnp.float32, least / len(shards), top_value / len(shards)))
        loudness = loudness * jnp.repeat(draws, extent[dim] // parts).reshape([-1 if axis == dim else 1 for axis in range(len(extent))])
    return loudness


def centred(key, dims, spread, limit, shards=(), kind=jnp.bfloat16):
    drawn = spread * jax.random.normal(key, dims, jnp.float32)
    if shards:
        drawn = drawn * steps_of(key, dims, shards, -0.22, 0.18)
    return jnp.clip(drawn, -limit, limit).astype(kind)


def gaussian_with(stream_key, dims, deviation, reach, cuts, heavy, dtype=jnp.bfloat16):
    result = deviation * jax.random.normal(stream_key, dims, jnp.float32)
    if cuts:
        result = result * steps_of(stream_key, dims, cuts, -0.22, 0.18)
    return jnp.clip(spiked(result, jax.random.fold_in(stream_key, 3), *heavy), -reach, reach).astype(dtype)


def setup_inputs(seed: int = 0) -> dict:
    key_of = jax.random.split(jax.random.key(seed), 5)
    front_rows = centred(key_of[0], (N_ROW * SLOTS, BLK, W), M ** -0.5, 0.109375, ((0, 8), (1, 4)))
    slot_blocks = draw_slot_blocks(jax.random.fold_in(key_of[4], 71), 0)
    inv_factor = draw_inv_factor(jax.random.fold_in(key_of[4], 71), 0)
    ancestor_inv = gaussian_with(key_of[3], (M, PANEL_ROWS * N_COL), 1.0, 6.0, ((0, 8), (1, 4)), (1, 0, 8, 2.0), jnp.float32)
    return dict(front_rows=front_rows, slot_blocks=slot_blocks, inv_factor=inv_factor, ancestor_inv=ancestor_inv)


def reference(front_rows, slot_blocks, inv_factor, ancestor_inv):
    nblocks = M // BLK
    target_rows = jnp.where(slot_blocks >= 0, slot_blocks, nblocks).astype(jnp.int32)
    placed = jnp.zeros((nblocks + 1, BLK, W), jnp.bfloat16).at[target_rows].set(front_rows)[:nblocks]
    lower_rows = placed.reshape(M, W).astype(jnp.float32)
    scaled = jnp.dot(lower_rows, inv_factor, precision=lax.Precision.HIGHEST, preferred_element_type=jnp.float32).astype(jnp.bfloat16)
    scaled_full = scaled.astype(jnp.float32)
    product = jnp.dot(ancestor_inv, scaled_full, precision=lax.Precision.HIGHEST, preferred_element_type=jnp.float32)
    gram_total = jnp.dot(scaled_full.T, product, precision=lax.Precision.HIGHEST, preferred_element_type=jnp.float32)
    factor_gram = jnp.dot(inv_factor.T, inv_factor, precision=lax.Precision.HIGHEST, preferred_element_type=jnp.float32)
    return -product, factor_gram + gram_total
```

```python
import functools

import jax
import jax.numpy as jnp
from jax import lax
from jax.experimental import pallas as pl
from jax.experimental.pallas import tpu as pltpu
from jax.sharding import PartitionSpec as P

MESH = pl.DeviceIdType.MESH
F32 = jnp.float32
BF16 = jnp.bfloat16


def split(x):
    high = x.astype(BF16)
    return high, (x - high.astype(F32)).astype(BF16)


def dot(a, b):
    return jnp.dot(a, b, preferred_element_type=F32)


def tdot(a, b):
    return lax.dot_general(a, b, (((0,), (0,)), ((), ())), preferred_element_type=F32)


def kernel(
    n_row, n_col, front, slots, factor_hbm, anc_hbm, out, diag,
    factor, anc, ids, pieces, blocks, perm, acc, part, part_in, own_rows, spread,
    gram, fgram, row_out, row_in, col_out, col_in, total_out, total_in,
    load_sem, ids_s, ids_r, a_s, a_r, b_s, b_r, f_s, c_s, c_r, w_s, w_r,
    gr_s, gr_r, gc_s, gc_r, gg_s, gg_r, gf_s,
):
    row = lax.axis_index("row")
    col = lax.axis_index("col")
    slot_count, height, width = front.shape
    block_height = height * n_col
    tile_rows, panel_rows = anc.shape
    panel_blocks = panel_rows // block_height
    share = tile_rows // n_col
    piece = row_out.shape[2]
    partner = row + 1 - 2 * lax.rem(row, 2)

    def row_peer(step):
        return lax.rem(row + step, n_row)

    def col_peer(step):
        return lax.rem(col + step, n_col)

    def copy(src, dst, s_sem, r_sem, to_row, to_col):
        return pltpu.make_async_remote_copy(
            src_ref=src, dst_ref=dst, send_sem=s_sem, recv_sem=r_sem,
            device_id=(to_row, to_col), device_id_type=MESH,
        )

    barrier = pltpu.get_barrier_semaphore()
    for step in range(1, n_row):
        pl.semaphore_signal(barrier, inc=1, device_id=(row_peer(step), col), device_id_type=MESH)
    for step in range(1, n_col):
        pl.semaphore_signal(barrier, inc=1, device_id=(row, col_peer(step)), device_id_type=MESH)
    load_factor = pltpu.make_async_copy(factor_hbm, factor, load_sem.at[0])
    load_anc = pltpu.make_async_copy(anc_hbm, anc, load_sem.at[1])
    load_factor.start()
    load_anc.start()

    number = jnp.int32(0)
    for s in range(slot_count):
        local = slots[s] - col * panel_blocks
        number = number + jnp.where((local >= 0) & (local < panel_blocks), local + 1, 0)
    ids[row] = jnp.full(ids.shape[1:], number - 1, jnp.int32)

    picked = []
    rows_in = [front[s].astype(F32) for s in range(slot_count)]
    for p in range(n_col):
        chosen = jnp.zeros((height, width), F32)
        for s in range(slot_count):
            local = slots[s] - p * panel_blocks
            keep = jnp.where((local >= 0) & (local < panel_blocks), 1.0, 0.0)
            chosen = chosen + rows_in[s] * keep
        picked.append(chosen)
    picked = jnp.concatenate(picked, axis=0).astype(BF16)
    load_factor.wait()
    f_high, f_low = split(factor[...])
    scaled = dot(picked, f_high) + dot(picked, f_low)
    for p in range(n_col):
        pieces[p] = scaled[p * height:(p + 1) * height].astype(BF16)
    blocks[row, col] = pieces[col]
    pl.semaphore_wait(barrier, n_row + n_col - 2)

    def a_copy(peer, there):
        return copy(pieces.at[peer], blocks.at[row, there], a_s.at[peer], a_r.at[there], row, peer)

    for step in range(1, n_col):
        a_copy(col_peer(step), col).start()

    def id_copy(peer, there):
        return copy(ids.at[there], ids.at[there], ids_s.at[peer], ids_r.at[there], peer, col)

    for step in range(1, n_row):
        id_copy(row_peer(step), row).start()
    load_anc.wait()
    for step in range(1, n_row):
        id_copy(row_peer(step), row_peer(step)).wait_recv()
    for step in range(1, n_col):
        a_copy(col_peer(step), col_peer(step)).wait_recv()

    def b_copy(peer, there):
        return copy(blocks.at[there], blocks.at[there], b_s.at[peer], b_r.at[there], peer, col)

    def b_forward(there):
        return copy(blocks.at[there], blocks.at[there], f_s.at[there], b_r.at[there], partner, col)

    for step in range(2, n_row, 2):
        b_copy(row_peer(step), row).start()
    b_copy(partner, row).start()

    @pl.loop(0, n_row)
    def _(m):
        mask_ids = ids[m, 0:1, 0:block_height]
        total = jnp.zeros((tile_rows, block_height), F32)
        for b in range(panel_blocks):
            keep = jnp.where(mask_ids == b, 1.0, 0.0)
            total = total + anc[:, b * block_height:(b + 1) * block_height] * keep
        perm[m] = total.astype(BF16)

    def block_of(m):
        if height % 16 == 0:
            return blocks[m].reshape(block_height, width)
        return blocks[m].astype(F32).reshape(block_height, width).astype(BF16)

    acc[...] = dot(perm[row], block_of(row))
    f_high, f_low = split(factor[...])
    fgram[...] = tdot(f_high, f_high) + tdot(f_high, f_low) + tdot(f_low, f_high)
    for step in range(2, n_row, 2):
        m = row_peer(n_row - step)
        b_copy(m, m).wait_recv()
        b_forward(m).start()
        acc[...] += dot(perm[m], block_of(m))
    for step in range(0, n_row, 2):
        m = lax.rem(partner + n_row - step, n_row)
        b_copy(m, m).wait_recv()
        acc[...] += dot(perm[m], block_of(m))

    for p in range(n_col):
        part[p] = acc[p * share:(p + 1) * share, :].astype(BF16)

    def c_copy(peer, there):
        return copy(part.at[peer], part_in.at[there], c_s.at[peer], c_r.at[there], row, peer)

    for step in range(1, n_col):
        c_copy(col_peer(step), col).start()

    root = row * n_col // n_row
    first = (row * tile_rows - root * panel_rows) // block_height

    def w_copy(peer):
        return copy(spread.at[peer], own_rows, w_s.at[peer], w_r.at[0], row, peer)

    @pl.when(col == root)
    def _():
        rows = []
        for i in range(tile_rows // block_height):
            chosen = jnp.zeros((block_height, width), F32)
            for m in range(n_row):
                keep = jnp.where(ids[m, 0:1, :] == first + i, 1.0, 0.0)
                chosen = chosen + block_of(m).astype(F32) * keep
            rows.append(chosen)
        rows = jnp.concatenate(rows, axis=0)
        for p in range(n_col):
            spread[p] = rows[p * share:(p + 1) * share].astype(BF16)
        for step in range(1, n_col):
            w_copy(col_peer(step)).start()
        own_rows[...] = spread[col]

    total = acc[pl.ds(pl.multiple_of(col * share, 8), share), :]
    for step in range(1, n_col):
        m = col_peer(step)
        c_copy(m, m).wait_recv()
        total = total + part_in[m].astype(F32)
    out[...] = -total

    @pl.when(col != root)
    def _():
        w_copy(root).wait_recv()

    t_high, t_low = split(total)
    mine = own_rows[...]
    gram[...] = tdot(mine, t_high) + tdot(mine, t_low)
    for j in range(n_row):
        for p in range(n_col):
            start = (p * n_row + j) * piece
            row_out[j, p] = gram[start:start + piece, :].astype(row_out.dtype)

    def gr_copy(peer, there):
        return copy(row_out.at[peer], row_in.at[there], gr_s.at[peer], gr_r.at[there], peer, col)

    for step in range(1, n_row):
        gr_copy(row_peer(step), row).start()
    summed = row_out[row].astype(F32)
    for step in range(1, n_row):
        m = row_peer(n_row - step)
        gr_copy(m, m).wait_recv()
        summed = summed + row_in[m].astype(F32)
    col_out[...] = summed

    def gc_copy(peer, there):
        return copy(col_out.at[peer], col_in.at[there], gc_s.at[peer], gc_r.at[there], row, peer)

    for step in range(1, n_col):
        gc_copy(col_peer(step), col).start()
    final = col_out[col]
    for step in range(1, n_col):
        m = col_peer(n_col - step)
        gc_copy(m, m).wait_recv()
        final = final + col_in[m]
    total_in[row] = final

    def gg_copy(peer, there):
        return copy(total_in.at[there], total_in.at[there], gg_s.at[peer], gg_r.at[there], peer, col)

    for step in range(1, n_row):
        gg_copy(row_peer(step), row).start()
    for step in range(1, n_row):
        m = row_peer(n_row - step)
        gg_copy(m, m).wait_recv()
    width_out = diag.shape[0]
    gathered = jnp.concatenate([total_in[m] for m in range(n_row)], axis=0)
    diag[...] = gathered + fgram[pl.ds(pl.multiple_of(col * width_out, 8), width_out), :]

    for step in range(1, n_col):
        peer = col_peer(step)
        a_copy(peer, col).wait_send()
        c_copy(peer, col).wait_send()
        gc_copy(peer, col).wait_send()
    for step in range(1, n_row):
        peer = row_peer(step)
        id_copy(peer, row).wait_send()
        gr_copy(peer, row).wait_send()
        gg_copy(peer, row).wait_send()
    for step in range(2, n_row, 2):
        b_copy(row_peer(step), row).wait_send()
        b_forward(row_peer(n_row - step)).wait_send()
    b_copy(partner, row).wait_send()

    @pl.when(col == root)
    def _():
        for step in range(1, n_col):
            w_copy(col_peer(step)).wait_send()


def solution(mesh):
    n_row, n_col = mesh.shape["row"], mesh.shape["col"]

    def body(front_rows, slot_blocks, inv_factor, ancestor_inv):
        _, height, width = front_rows.shape
        tile_rows, panel_rows = ancestor_inv.shape
        block_height = height * n_col
        share = tile_rows // n_col
        diag_width = width // n_col
        piece = diag_width // n_row
        wire = BF16 if piece % 16 == 0 else F32
        vmem = pltpu.VMEM
        dma = pltpu.SemaphoreType.DMA
        return pl.pallas_call(
            functools.partial(kernel, n_row, n_col),
            out_shape=(
                jax.ShapeDtypeStruct((share, width), F32),
                jax.ShapeDtypeStruct((diag_width, width), F32),
            ),
            in_specs=[
                pl.BlockSpec(memory_space=pltpu.VMEM),
                pl.BlockSpec(memory_space=pltpu.SMEM),
                pl.BlockSpec(memory_space=pl.ANY),
                pl.BlockSpec(memory_space=pl.ANY),
            ],
            out_specs=(
                pl.BlockSpec(memory_space=pltpu.VMEM),
                pl.BlockSpec(memory_space=pltpu.VMEM),
            ),
            scratch_shapes=[
                vmem((width, width), F32),
                vmem((tile_rows, panel_rows), F32),
                vmem((n_row, 8, width), jnp.int32),
                vmem((n_col, height, width), BF16),
                vmem((n_row, n_col, height, width), BF16),
                vmem((n_row, tile_rows, block_height), BF16),
                vmem((tile_rows, width), F32),
                vmem((n_col, share, width), BF16),
                vmem((n_col, share, width), BF16),
                vmem((share, width), BF16),
                vmem((n_col, share, width), BF16),
                vmem((width, width), F32),
                vmem((width, width), F32),
                vmem((n_row, n_col, piece, width), wire),
                vmem((n_row, n_col, piece, width), wire),
                vmem((n_col, piece, width), F32),
                vmem((n_col, piece, width), F32),
                vmem((n_row, piece, width), F32),
                vmem((n_row, piece, width), F32),
                dma((2,)),
                dma((n_row,)), dma((n_row,)),
                dma((n_col,)), dma((n_col,)),
                dma((n_row,)), dma((n_row,)), dma((n_row,)),
                dma((n_col,)), dma((n_col,)),
                dma((n_col,)), dma((1,)),
                dma((n_row,)), dma((n_row,)),
                dma((n_col,)), dma((n_col,)),
                dma((n_row,)), dma((n_row,)), dma((n_row,)),
            ],
            compiler_params=pltpu.CompilerParams(
                collective_id=0, has_side_effects=True, vmem_limit_bytes=60 * 1024 * 1024
            ),
        )(front_rows, slot_blocks, inv_factor, ancestor_inv)

    in_specs = (P("row", "col", None), P("row"), P(), P("row", "col"))
    out_specs = (P(("row", "col"), None), P("col", None))
    return jax.shard_map(body, mesh=mesh, in_specs=in_specs, out_specs=out_specs, check_vma=False)
```

```python
import functools

import jax
import jax.numpy as jnp
from jax import lax
from jax.experimental import pallas as pl
from jax.experimental.pallas import tpu as pltpu
from jax.sharding import PartitionSpec as P

MESH = pl.DeviceIdType.MESH
F32 = jnp.float32
BF16 = jnp.bfloat16


def split(x):
    high = x.astype(BF16)
    return high, (x - high.astype(F32)).astype(BF16)


def dot(a, b):
    return jnp.dot(a, b, preferred_element_type=F32)


def tdot(a, b):
    return lax.dot_general(a, b, (((0,), (0,)), ((), ())), preferred_element_type=F32)


def kernel(
    n_row, n_col, parts, front, slots, factor_hbm, anc_hbm, out, diag, fdiag,
    factor, anc, ids, pieces, blocks, perm, acc, part, part_in, own_rows, spread,
    gram, row_out, row_in, col_out, col_in, total_in,
    load_sem, ids_s, ids_r, a_s, a_r, b_s, b_r, f_s, c_s, c_r, w_s, w_r,
    gr_s, gr_r, gc_s, gc_r, gg_s, gg_r,
):
    row = lax.axis_index("row")
    col = lax.axis_index("col")
    slot_count, height, width = front.shape
    block_height = height * n_col
    tile_rows, panel_rows = anc.shape
    panel_blocks = panel_rows // block_height
    share = tile_rows // n_col
    piece = row_out.shape[3]
    part_width = width // parts
    partner = row + 1 - 2 * lax.rem(row, 2)

    def row_peer(step):
        return lax.rem(row + step, n_row)

    def col_peer(step):
        return lax.rem(col + step, n_col)

    def copy(src, dst, s_sem, r_sem, to_row, to_col):
        return pltpu.make_async_remote_copy(
            src_ref=src, dst_ref=dst, send_sem=s_sem, recv_sem=r_sem,
            device_id=(to_row, to_col), device_id_type=MESH,
        )

    barrier = pltpu.get_barrier_semaphore()
    for step in range(1, n_row):
        pl.semaphore_signal(barrier, inc=1, device_id=(row_peer(step), col), device_id_type=MESH)
    for step in range(1, n_col):
        pl.semaphore_signal(barrier, inc=1, device_id=(row, col_peer(step)), device_id_type=MESH)
    load_factor = pltpu.make_async_copy(factor_hbm, factor, load_sem.at[0])
    load_anc = pltpu.make_async_copy(anc_hbm, anc, load_sem.at[1])
    load_factor.start()
    load_anc.start()

    number = jnp.int32(0)
    for s in range(slot_count):
        local = slots[s] - col * panel_blocks
        number = number + jnp.where((local >= 0) & (local < panel_blocks), local + 1, 0)
    ids[row] = jnp.full(ids.shape[1:], number - 1, jnp.int32)

    picked = []
    rows_in = [front[s].astype(F32) for s in range(slot_count)]
    for p in range(n_col):
        chosen = jnp.zeros((height, width), F32)
        for s in range(slot_count):
            local = slots[s] - p * panel_blocks
            keep = jnp.where((local >= 0) & (local < panel_blocks), 1.0, 0.0)
            chosen = chosen + rows_in[s] * keep
        picked.append(chosen)
    picked = jnp.concatenate(picked, axis=0).astype(BF16)
    load_factor.wait()
    f_high, f_low = split(factor[...])
    scaled = dot(picked, f_high) + dot(picked, f_low)
    for h in range(parts):
        for p in range(n_col):
            piece_rows = scaled[p * height:(p + 1) * height, h * part_width:(h + 1) * part_width]
            pieces[h, p] = piece_rows.astype(BF16)
        blocks[h, row, col] = pieces[h, col]
    pl.semaphore_wait(barrier, n_row + n_col - 2)

    def a_copy(h, peer, there):
        return copy(
            pieces.at[h, peer], blocks.at[h, row, there], a_s.at[h, peer], a_r.at[h, there], row, peer
        )

    def id_copy(peer, there):
        return copy(ids.at[there], ids.at[there], ids_s.at[peer], ids_r.at[there], peer, col)

    for h in range(parts):
        for step in range(1, n_col):
            a_copy(h, col_peer(step), col).start()
        if h == 0:
            for step in range(1, n_row):
                id_copy(row_peer(step), row).start()

    def b_copy(h, peer, there):
        return copy(
            blocks.at[h, there], blocks.at[h, there], b_s.at[h, peer], b_r.at[h, there], peer, col
        )

    def b_forward(h, there):
        return copy(
            blocks.at[h, there], blocks.at[h, there], f_s.at[h, there], b_r.at[h, there], partner, col
        )

    for h in range(parts):
        for step in range(1, n_col):
            a_copy(h, col_peer(step), col_peer(step)).wait_recv()
        for step in range(2, n_row, 2):
            b_copy(h, row_peer(step), row).start()
        b_copy(h, partner, row).start()

    for step in range(1, n_row):
        id_copy(row_peer(step), row_peer(step)).wait_recv()
    load_anc.wait()

    @pl.loop(0, n_row)
    def _(m):
        mask_ids = ids[m, 0:1, 0:block_height]
        total = jnp.zeros((tile_rows, block_height), F32)
        for b in range(panel_blocks):
            keep = jnp.where(mask_ids == b, 1.0, 0.0)
            total = total + anc[:, b * block_height:(b + 1) * block_height] * keep
        perm[m] = total.astype(BF16)

    def block_of(h, m):
        if height % 16 == 0:
            return blocks[h, m].reshape(block_height, part_width)
        return blocks[h, m].astype(F32).reshape(block_height, part_width).astype(BF16)

    root = row * n_col // n_row
    first = (row * tile_rows - root * panel_rows) // block_height

    def c_copy(h, peer, there):
        return copy(
            part.at[h, peer], part_in.at[h, there], c_s.at[h, peer], c_r.at[h, there], row, peer
        )

    def w_copy(h, peer):
        return copy(spread.at[h, peer], own_rows.at[h], w_s.at[h, peer], w_r.at[h], row, peer)

    def send_sums(h):
        for p in range(n_col):
            part[h, p] = acc[h, p * share:(p + 1) * share, :].astype(BF16)
        for step in range(1, n_col):
            c_copy(h, col_peer(n_col - step), col).start()

    def send_rows(h):
        @pl.when(col == root)
        def _():
            rows = []
            for i in range(tile_rows // block_height):
                chosen = jnp.zeros((block_height, part_width), F32)
                for m in range(n_row):
                    keep = jnp.where(ids[m, 0:1, 0:part_width] == first + i, 1.0, 0.0)
                    chosen = chosen + block_of(h, m).astype(F32) * keep
                rows.append(chosen)
            rows = jnp.concatenate(rows, axis=0)
            for p in range(n_col):
                spread[h, p] = rows[p * share:(p + 1) * share].astype(BF16)
            for step in range(1, n_col):
                w_copy(h, col_peer(step)).start()
            own_rows[h] = spread[h, col]

    for h in range(parts):
        acc[h] = dot(perm[row], block_of(h, row))
        for step in range(2, n_row, 2):
            m = row_peer(n_row - step)
            b_copy(h, m, m).wait_recv()
            b_forward(h, m).start()
            acc[h] += dot(perm[m], block_of(h, m))
        for step in range(0, n_row, 2):
            m = lax.rem(partner + n_row - step, n_row)
            b_copy(h, m, m).wait_recv()
            acc[h] += dot(perm[m], block_of(h, m))
        if h < parts - 1:
            send_sums(h)
            send_rows(h)
        else:
            send_rows(h)
            send_sums(h)

    f_high, f_low = split(factor[...])
    gram[...] = tdot(f_high, f_high) + tdot(f_high, f_low) + tdot(f_low, f_high)
    width_out = diag.shape[0]
    fdiag[...] = gram[pl.ds(pl.multiple_of(col * width_out, 8), width_out), :]

    def gr_copy(h, peer, there):
        return copy(
            row_out.at[h, peer], row_in.at[h, there], gr_s.at[h, peer], gr_r.at[h, there], peer, col
        )

    def gc_copy(h, peer, there):
        return copy(
            col_out.at[h, peer], col_in.at[h, there], gc_s.at[h, peer], gc_r.at[h, there], row, peer
        )

    def gg_copy(h, peer, there):
        return copy(
            total_in.at[h, there], total_in.at[h, there], gg_s.at[h, peer], gg_r.at[h, there], peer, col
        )

    for h in range(parts):
        lanes = slice(h * part_width, (h + 1) * part_width)
        total = acc[h, pl.ds(pl.multiple_of(col * share, 8), share), :]
        for step in range(1, n_col):
            m = col_peer(step)
            c_copy(h, m, m).wait_recv()
            total = total + part_in[h, m].astype(F32)
        out[:, lanes] = total
        t_high, t_low = split(total)
        for g in range(parts):
            if h == 0:
                @pl.when(col != root)
                def _():
                    w_copy(g, root).wait_recv()
            mine = own_rows[g]
            rows_g = slice(g * part_width, (g + 1) * part_width)
            gram[rows_g, lanes] = tdot(mine, t_high) + tdot(mine, t_low)
        for j in range(n_row):
            for p in range(n_col):
                start = (p * n_row + j) * piece
                row_out[h, j, p] = gram[start:start + piece, lanes].astype(row_out.dtype)
        for step in range(1, n_row):
            gr_copy(h, row_peer(step), row).start()

    for h in range(parts):
        summed = row_out[h, row].astype(F32)
        for step in range(1, n_row):
            m = row_peer(n_row - step)
            gr_copy(h, m, m).wait_recv()
            summed = summed + row_in[h, m].astype(F32)
        col_out[h] = summed
        for step in range(1, n_col):
            gc_copy(h, col_peer(step), col).start()

    for h in range(parts):
        final = col_out[h, col]
        for step in range(1, n_col):
            m = col_peer(n_col - step)
            gc_copy(h, m, m).wait_recv()
            final = final + col_in[h, m]
        total_in[h, row] = final
        for step in range(1, n_row):
            gg_copy(h, row_peer(step), row).start()

    for h in range(parts):
        for step in range(1, n_row):
            m = row_peer(n_row - step)
            gg_copy(h, m, m).wait_recv()
        gathered = jnp.concatenate([total_in[h, m] for m in range(n_row)], axis=0)
        diag[:, h * part_width:(h + 1) * part_width] = gathered

    for h in range(parts):
        for step in range(1, n_col):
            peer = col_peer(step)
            a_copy(h, peer, col).wait_send()
            c_copy(h, peer, col).wait_send()
            gc_copy(h, peer, col).wait_send()
        for step in range(1, n_row):
            peer = row_peer(step)
            if h == 0:
                id_copy(peer, row).wait_send()
            gr_copy(h, peer, row).wait_send()
            gg_copy(h, peer, row).wait_send()
        for step in range(2, n_row, 2):
            b_copy(h, row_peer(step), row).wait_send()
            b_forward(h, row_peer(n_row - step)).wait_send()
        b_copy(h, partner, row).wait_send()

    @pl.when(col == root)
    def _():
        for h in range(parts):
            for step in range(1, n_col):
                w_copy(h, col_peer(step)).wait_send()


PARTS = 2


def solution(mesh):
    n_row, n_col = mesh.shape["row"], mesh.shape["col"]

    def body(front_rows, slot_blocks, inv_factor, ancestor_inv):
        _, height, width = front_rows.shape
        tile_rows, panel_rows = ancestor_inv.shape
        block_height = height * n_col
        share = tile_rows // n_col
        diag_width = width // n_col
        piece = diag_width // n_row
        parts, part_width = PARTS, width // PARTS
        wire = BF16 if piece % 16 == 0 else F32
        vmem = pltpu.VMEM

        def dma(*shape):
            return pltpu.SemaphoreType.DMA(shape)

        in_vmem = pl.BlockSpec(memory_space=pltpu.VMEM)
        anywhere = pl.BlockSpec(memory_space=pl.ANY)
        total, gram, factor_gram = pl.pallas_call(
            functools.partial(kernel, n_row, n_col, parts),
            out_shape=(
                jax.ShapeDtypeStruct((share, width), F32),
                jax.ShapeDtypeStruct((diag_width, width), F32),
                jax.ShapeDtypeStruct((diag_width, width), F32),
            ),
            in_specs=[in_vmem, pl.BlockSpec(memory_space=pltpu.SMEM), anywhere, anywhere],
            out_specs=(in_vmem, in_vmem, in_vmem),
            scratch_shapes=[
                vmem((width, width), F32),
                vmem((tile_rows, panel_rows), F32),
                vmem((n_row, 8, max(part_width, block_height)), jnp.int32),
                vmem((parts, n_col, height, part_width), BF16),
                vmem((parts, n_row, n_col, height, part_width), BF16),
                vmem((n_row, tile_rows, block_height), BF16),
                vmem((parts, tile_rows, part_width), F32),
                vmem((parts, n_col, share, part_width), BF16),
                vmem((parts, n_col, share, part_width), BF16),
                vmem((parts, share, part_width), BF16),
                vmem((parts, n_col, share, part_width), BF16),
                vmem((width, width), F32),
                vmem((parts, n_row, n_col, piece, part_width), wire),
                vmem((parts, n_row, n_col, piece, part_width), wire),
                vmem((parts, n_col, piece, part_width), F32),
                vmem((parts, n_col, piece, part_width), F32),
                vmem((parts, n_row, piece, part_width), F32),
                dma(2),
                dma(n_row), dma(n_row),
                dma(parts, n_col), dma(parts, n_col),
                dma(parts, n_row), dma(parts, n_row), dma(parts, n_row),
                dma(parts, n_col), dma(parts, n_col),
                dma(parts, n_col), dma(parts),
                dma(parts, n_row), dma(parts, n_row),
                dma(parts, n_col), dma(parts, n_col),
                dma(parts, n_row), dma(parts, n_row),
            ],
            compiler_params=pltpu.CompilerParams(
                collective_id=0, has_side_effects=True, vmem_limit_bytes=60 * 1024 * 1024
            ),
        )(front_rows, slot_blocks, inv_factor, ancestor_inv)
        return -total, factor_gram + gram

    in_specs = (P("row", "col", None), P("row"), P(), P("row", "col"))
    out_specs = (P(("row", "col"), None), P("col", None))
    return jax.shard_map(body, mesh=mesh, in_specs=in_specs, out_specs=out_specs, check_vma=False)
```

```python
import functools

import jax
import jax.numpy as jnp
from jax import lax
from jax.experimental import pallas as pl
from jax.experimental.pallas import tpu as pltpu
from jax.sharding import PartitionSpec as P

MESH = pl.DeviceIdType.MESH
F32 = jnp.float32
BF16 = jnp.bfloat16


def split(x):
    high = x.astype(BF16)
    return high, (x - high.astype(F32)).astype(BF16)


def dot(a, b):
    return jnp.dot(a, b, preferred_element_type=F32)


def tdot(a, b):
    return lax.dot_general(a, b, (((0,), (0,)), ((), ())), preferred_element_type=F32)


def kernel(
    n_row, n_col, parts, front, slots, factor_hbm, anc_hbm, out, diag, fdiag,
    factor, anc, ids, pieces, blocks, perm, acc, part, part_in, own_rows, spread,
    gram, row_out, row_in, col_out, col_in, total_in,
    load_sem, ids_s, ids_r, a_s, a_r, b_s, b_r, f_s, c_s, c_r, w_s, w_r,
    gr_s, gr_r, gc_s, gc_r, gg_s, gg_r,
):
    row = lax.axis_index("row")
    col = lax.axis_index("col")
    slot_count, height, width = front.shape
    block_height = height * n_col
    tile_rows, panel_rows = anc.shape
    panel_blocks = panel_rows // block_height
    share = tile_rows // n_col
    piece = row_out.shape[3]
    part_width = width // parts
    partner = row + 1 - 2 * lax.rem(row, 2)
    half = n_row // 2

    def place(m):
        return lax.rem(m, 2) * half + m // 2

    def row_peer(step):
        return lax.rem(row + step, n_row)

    def col_peer(step):
        return lax.rem(col + step, n_col)

    def copy(src, dst, s_sem, r_sem, to_row, to_col):
        return pltpu.make_async_remote_copy(
            src_ref=src, dst_ref=dst, send_sem=s_sem, recv_sem=r_sem,
            device_id=(to_row, to_col), device_id_type=MESH,
        )

    barrier = pltpu.get_barrier_semaphore()
    for step in range(1, n_row):
        pl.semaphore_signal(barrier, inc=1, device_id=(row_peer(step), col), device_id_type=MESH)
    for step in range(1, n_col):
        pl.semaphore_signal(barrier, inc=1, device_id=(row, col_peer(step)), device_id_type=MESH)
    load_factor = pltpu.make_async_copy(factor_hbm, factor, load_sem.at[0])
    load_anc = pltpu.make_async_copy(anc_hbm, anc, load_sem.at[1])
    load_factor.start()
    load_anc.start()

    number = jnp.int32(0)
    for s in range(slot_count):
        local = slots[s] - col * panel_blocks
        number = number + jnp.where((local >= 0) & (local < panel_blocks), local + 1, 0)
    ids[row] = jnp.full(ids.shape[1:], number - 1, jnp.int32)

    picked = []
    rows_in = [front[s].astype(F32) for s in range(slot_count)]
    for p in range(n_col):
        chosen = jnp.zeros((height, width), F32)
        for s in range(slot_count):
            local = slots[s] - p * panel_blocks
            keep = jnp.where((local >= 0) & (local < panel_blocks), 1.0, 0.0)
            chosen = chosen + rows_in[s] * keep
        picked.append(chosen)
    picked = jnp.concatenate(picked, axis=0).astype(BF16)
    load_factor.wait()
    f_high, f_low = split(factor[...])
    scaled = dot(picked, f_high) + dot(picked, f_low)
    for h in range(parts):
        for p in range(n_col):
            piece_rows = scaled[p * height:(p + 1) * height, h * part_width:(h + 1) * part_width]
            pieces[h, p] = piece_rows.astype(BF16)
        blocks[h, place(row), col] = pieces[h, col]
    pl.semaphore_wait(barrier, n_row + n_col - 2)

    def a_copy(h, peer, there):
        return copy(
            pieces.at[h, peer], blocks.at[h, place(row), there], a_s.at[h, peer], a_r.at[h, there], row, peer
        )

    def id_copy(peer, there):
        return copy(ids.at[there], ids.at[there], ids_s.at[peer], ids_r.at[there], peer, col)

    for h in range(parts):
        for step in range(1, n_col):
            a_copy(h, col_peer(step), col).start()
        if h == 0:
            for step in range(1, n_row):
                id_copy(row_peer(step), row).start()

    def b_copy(h, peer, there):
        return copy(
            blocks.at[h, place(there)], blocks.at[h, place(there)], b_s.at[h, peer], b_r.at[h, there], peer, col
        )

    def b_forward(h, there):
        return copy(
            blocks.at[h, place(there)], blocks.at[h, place(there)], f_s.at[h, there], b_r.at[h, there], partner, col
        )

    for h in range(parts):
        for step in range(1, n_col):
            a_copy(h, col_peer(step), col_peer(step)).wait_recv()
        for step in range(2, n_row, 2):
            b_copy(h, row_peer(step), row).start()
        b_copy(h, partner, row).start()

    for step in range(1, n_row):
        id_copy(row_peer(step), row_peer(step)).wait_recv()
    load_anc.wait()

    for side in range(2):
        @pl.loop(0, half)
        def _(q):
            mask_ids = ids[2 * q + side, 0:1, 0:block_height]
            total = jnp.zeros((tile_rows, block_height), F32)
            for b in range(panel_blocks):
                keep = jnp.where(mask_ids == b, 1.0, 0.0)
                total = total + anc[:, b * block_height:(b + 1) * block_height] * keep
            lanes = pl.ds(pl.multiple_of(q * block_height, block_height), block_height)
            perm[side, :, lanes] = total.astype(BF16)

    def block_of(h, m, count=1):
        held = blocks[h, pl.ds(m, count)]
        if height % 16 == 0:
            return held.reshape(count * block_height, part_width)
        return held.astype(F32).reshape(count * block_height, part_width).astype(BF16)

    def half_product(h, side):
        return dot(perm[side], block_of(h, side * half, half))

    root = row * n_col // n_row
    first = (row * tile_rows - root * panel_rows) // block_height

    def c_copy(h, peer, there):
        return copy(
            part.at[h, peer], part_in.at[h, there], c_s.at[h, peer], c_r.at[h, there], row, peer
        )

    def w_copy(h, peer):
        return copy(spread.at[h, peer], own_rows.at[h], w_s.at[h, peer], w_r.at[h], row, peer)

    def send_sums(h):
        for p in range(n_col):
            part[h, p] = acc[h, p * share:(p + 1) * share, :].astype(BF16)
        for step in range(1, n_col):
            c_copy(h, col_peer(n_col - step), col).start()

    def send_rows(h):
        @pl.when(col == root)
        def _():
            rows = []
            for i in range(tile_rows // block_height):
                chosen = jnp.zeros((block_height, part_width), F32)
                for m in range(n_row):
                    keep = jnp.where(ids[m, 0:1, 0:part_width] == first + i, 1.0, 0.0)
                    chosen = chosen + block_of(h, (m % 2) * half + m // 2).astype(F32) * keep
                rows.append(chosen)
            rows = jnp.concatenate(rows, axis=0)
            for p in range(n_col):
                spread[h, p] = rows[p * share:(p + 1) * share].astype(BF16)
            for step in range(1, n_col):
                w_copy(h, col_peer(step)).start()
            own_rows[h] = spread[h, col]

    for h in range(parts):
        for step in range(2, n_row, 2):
            m = row_peer(n_row - step)
            b_copy(h, m, m).wait_recv()
            b_forward(h, m).start()
        acc[h] = half_product(h, lax.rem(row, 2))
        for step in range(0, n_row, 2):
            m = lax.rem(partner + n_row - step, n_row)
            b_copy(h, m, m).wait_recv()
        acc[h] += half_product(h, lax.rem(partner, 2))
        if h < parts - 1:
            send_sums(h)
            send_rows(h)
        else:
            send_rows(h)
            send_sums(h)

    f_high, f_low = split(factor[...])
    gram[...] = tdot(f_high, f_high) + tdot(f_high, f_low) + tdot(f_low, f_high)
    width_out = diag.shape[0]
    fdiag[...] = gram[pl.ds(pl.multiple_of(col * width_out, 8), width_out), :]

    def gr_copy(h, peer, there):
        return copy(
            row_out.at[h, peer], row_in.at[h, there], gr_s.at[h, peer], gr_r.at[h, there], peer, col
        )

    def gc_copy(h, peer, there):
        return copy(
            col_out.at[h, peer], col_in.at[h, there], gc_s.at[h, peer], gc_r.at[h, there], row, peer
        )

    def gg_copy(h, peer, there):
        return copy(
            total_in.at[h, there], total_in.at[h, there], gg_s.at[h, peer], gg_r.at[h, there], peer, col
        )

    for h in range(parts):
        lanes = slice(h * part_width, (h + 1) * part_width)
        total = acc[h, pl.ds(pl.multiple_of(col * share, 8), share), :]
        for step in range(1, n_col):
            m = col_peer(step)
            c_copy(h, m, m).wait_recv()
            total = total + part_in[h, m].astype(F32)
        out[:, lanes] = total
        t_high, t_low = split(total)
        for g in range(parts):
            if h == 0:
                @pl.when(col != root)
                def _():
                    w_copy(g, root).wait_recv()
            mine = own_rows[g]
            rows_g = slice(g * part_width, (g + 1) * part_width)
            gram[rows_g, lanes] = tdot(mine, t_high) + tdot(mine, t_low)
        for j in range(n_row):
            for p in range(n_col):
                start = (p * n_row + j) * piece
                row_out[h, j, p] = gram[start:start + piece, lanes].astype(row_out.dtype)
        for step in range(1, n_row):
            gr_copy(h, row_peer(step), row).start()

    for h in range(parts):
        summed = row_out[h, row].astype(F32)
        for step in range(1, n_row):
            m = row_peer(n_row - step)
            gr_copy(h, m, m).wait_recv()
            summed = summed + row_in[h, m].astype(F32)
        col_out[h] = summed
        for step in range(1, n_col):
            gc_copy(h, col_peer(step), col).start()

    for h in range(parts):
        final = col_out[h, col]
        for step in range(1, n_col):
            m = col_peer(n_col - step)
            gc_copy(h, m, m).wait_recv()
            final = final + col_in[h, m]
        total_in[h, row] = final
        for step in range(1, n_row):
            gg_copy(h, row_peer(step), row).start()

    for h in range(parts):
        for step in range(1, n_row):
            m = row_peer(n_row - step)
            gg_copy(h, m, m).wait_recv()
        gathered = jnp.concatenate([total_in[h, m] for m in range(n_row)], axis=0)
        diag[:, h * part_width:(h + 1) * part_width] = gathered

    for h in range(parts):
        for step in range(1, n_col):
            peer = col_peer(step)
            a_copy(h, peer, col).wait_send()
            c_copy(h, peer, col).wait_send()
            gc_copy(h, peer, col).wait_send()
        for step in range(1, n_row):
            peer = row_peer(step)
            if h == 0:
                id_copy(peer, row).wait_send()
            gr_copy(h, peer, row).wait_send()
            gg_copy(h, peer, row).wait_send()
        for step in range(2, n_row, 2):
            b_copy(h, row_peer(step), row).wait_send()
            b_forward(h, row_peer(n_row - step)).wait_send()
        b_copy(h, partner, row).wait_send()

    @pl.when(col == root)
    def _():
        for h in range(parts):
            for step in range(1, n_col):
                w_copy(h, col_peer(step)).wait_send()


PARTS = 2


def solution(mesh):
    n_row, n_col = mesh.shape["row"], mesh.shape["col"]

    def body(front_rows, slot_blocks, inv_factor, ancestor_inv):
        _, height, width = front_rows.shape
        tile_rows, panel_rows = ancestor_inv.shape
        block_height = height * n_col
        share = tile_rows // n_col
        diag_width = width // n_col
        piece = diag_width // n_row
        parts, part_width = PARTS, width // PARTS
        wire = BF16 if piece % 16 == 0 else F32
        vmem = pltpu.VMEM

        def dma(*shape):
            return pltpu.SemaphoreType.DMA(shape)

        in_vmem = pl.BlockSpec(memory_space=pltpu.VMEM)
        anywhere = pl.BlockSpec(memory_space=pl.ANY)
        total, gram, factor_gram = pl.pallas_call(
            functools.partial(kernel, n_row, n_col, parts),
            out_shape=(
                pltpu.VMEM((share, width), F32),
                pltpu.VMEM((diag_width, width), F32),
                pltpu.VMEM((diag_width, width), F32),
            ),
            in_specs=[in_vmem, pl.BlockSpec(memory_space=pltpu.SMEM), anywhere, anywhere],
            out_specs=(in_vmem, in_vmem, in_vmem),
            scratch_shapes=[
                vmem((width, width), F32),
                vmem((tile_rows, panel_rows), F32),
                vmem((n_row, 8, max(part_width, block_height)), jnp.int32),
                vmem((parts, n_col, height, part_width), BF16),
                vmem((parts, n_row, n_col, height, part_width), BF16),
                vmem((2, tile_rows, n_row // 2 * block_height), BF16),
                vmem((parts, tile_rows, part_width), F32),
                vmem((parts, n_col, share, part_width), BF16),
                vmem((parts, n_col, share, part_width), BF16),
                vmem((parts, share, part_width), BF16),
                vmem((parts, n_col, share, part_width), BF16),
                vmem((width, width), F32),
                vmem((parts, n_row, n_col, piece, part_width), wire),
                vmem((parts, n_row, n_col, piece, part_width), wire),
                vmem((parts, n_col, piece, part_width), F32),
                vmem((parts, n_col, piece, part_width), F32),
                vmem((parts, n_row, piece, part_width), F32),
                dma(2),
                dma(n_row), dma(n_row),
                dma(parts, n_col), dma(parts, n_col),
                dma(parts, n_row), dma(parts, n_row), dma(parts, n_row),
                dma(parts, n_col), dma(parts, n_col),
                dma(parts, n_col), dma(parts),
                dma(parts, n_row), dma(parts, n_row),
                dma(parts, n_col), dma(parts, n_col),
                dma(parts, n_row), dma(parts, n_row),
            ],
            compiler_params=pltpu.CompilerParams(
                collective_id=0, has_side_effects=True, vmem_limit_bytes=60 * 1024 * 1024
            ),
        )(front_rows, slot_blocks, inv_factor, ancestor_inv)
        return -total, factor_gram + gram

    in_specs = (P("row", "col", None), P("row"), P(), P("row", "col"))
    out_specs = (P(("row", "col"), None), P("col", None))
    return jax.shard_map(body, mesh=mesh, in_specs=in_specs, out_specs=out_specs, check_vma=False)
```

```python
import functools

import jax
import jax.numpy as jnp
from jax import lax
from jax.experimental import pallas as pl
from jax.experimental.pallas import tpu as pltpu
from jax.sharding import PartitionSpec as P

MESH = pl.DeviceIdType.MESH
F32 = jnp.float32
BF16 = jnp.bfloat16


def split(x):
    high = x.astype(BF16)
    return high, (x - high.astype(F32)).astype(BF16)


def dot(a, b):
    return jnp.dot(a, b, preferred_element_type=F32)


def tdot(a, b):
    return lax.dot_general(a, b, (((0,), (0,)), ((), ())), preferred_element_type=F32)


def kernel(
    n_row, n_col, parts, front, slots, factor_hbm, anc_hbm, out, diag, fdiag,
    factor, anc, ids, pieces, blocks, perm, acc, part, part_in, own_rows, spread,
    spare, gram, row_out, row_in, col_out, col_in, total_in,
    load_sem, ids_s, ids_r, a_s, a_r, b_s, b_r, f_s, c_s, c_r, w_s, w_r,
    gr_s, gr_r, gc_s, gc_r, gg_s, gg_r,
):
    row = lax.axis_index("row")
    col = lax.axis_index("col")
    slot_count, height, width = front.shape
    block_height = height * n_col
    tile_rows, panel_rows = anc.shape
    panel_blocks = panel_rows // block_height
    share = tile_rows // n_col
    piece = row_out.shape[3]
    part_width = width // parts
    partner = row + 1 - 2 * lax.rem(row, 2)
    half = n_row // 2

    def place(m):
        return lax.rem(m, 2) * half + m // 2

    def row_peer(step):
        return lax.rem(row + step, n_row)

    def col_peer(step):
        return lax.rem(col + step, n_col)

    def copy(src, dst, s_sem, r_sem, to_row, to_col):
        return pltpu.make_async_remote_copy(
            src_ref=src, dst_ref=dst, send_sem=s_sem, recv_sem=r_sem,
            device_id=(to_row, to_col), device_id_type=MESH,
        )

    barrier = pltpu.get_barrier_semaphore()
    for step in range(1, n_row):
        pl.semaphore_signal(barrier, inc=1, device_id=(row_peer(step), col), device_id_type=MESH)
    for step in range(1, n_col):
        pl.semaphore_signal(barrier, inc=1, device_id=(row, col_peer(step)), device_id_type=MESH)
    across = lax.rem(row + n_row // 2, n_row)
    own_root = row * n_col // n_row
    across_root = across * n_col // n_row

    @pl.when(col != own_root)
    def _():
        pl.semaphore_signal(barrier, inc=1, device_id=(across, own_root), device_id_type=MESH)

    load_factor = pltpu.make_async_copy(factor_hbm, factor, load_sem.at[0])
    load_anc = pltpu.make_async_copy(anc_hbm, anc, load_sem.at[1])
    load_factor.start()
    load_anc.start()

    number = jnp.int32(0)
    for s in range(slot_count):
        local = slots[s] - col * panel_blocks
        number = number + jnp.where((local >= 0) & (local < panel_blocks), local + 1, 0)
    ids[row] = jnp.full(ids.shape[1:], number - 1, jnp.int32)

    picked = []
    rows_in = [front[s].astype(F32) for s in range(slot_count)]
    for p in range(n_col):
        chosen = jnp.zeros((height, width), F32)
        for s in range(slot_count):
            local = slots[s] - p * panel_blocks
            keep = jnp.where((local >= 0) & (local < panel_blocks), 1.0, 0.0)
            chosen = chosen + rows_in[s] * keep
        picked.append(chosen)
    picked = jnp.concatenate(picked, axis=0).astype(BF16)
    load_factor.wait()
    f_high, f_low = split(factor[...])
    scaled = dot(picked, f_high) + dot(picked, f_low)
    for h in range(parts):
        for p in range(n_col):
            piece_rows = scaled[p * height:(p + 1) * height, h * part_width:(h + 1) * part_width]
            pieces[h, p] = piece_rows.astype(BF16)
        blocks[h, place(row), col] = pieces[h, col]
    extra = jnp.where(col == across_root, n_col - 1, 0)
    pl.semaphore_wait(barrier, n_row + n_col - 2 + extra)

    def a_copy(h, peer, there):
        return copy(
            pieces.at[h, peer], blocks.at[h, place(row), there], a_s.at[h, peer], a_r.at[h, there], row, peer
        )

    def id_copy(peer, there):
        return copy(ids.at[there], ids.at[there], ids_s.at[peer], ids_r.at[there], peer, col)

    for h in range(parts):
        for step in range(1, n_col):
            a_copy(h, col_peer(step), col).start()
        if h == 0:
            for step in range(1, n_row):
                id_copy(row_peer(step), row).start()

    def b_copy(h, peer, there):
        return copy(
            blocks.at[h, place(there)], blocks.at[h, place(there)], b_s.at[h, peer], b_r.at[h, there], peer, col
        )

    def b_forward(h, there):
        return copy(
            blocks.at[h, place(there)], blocks.at[h, place(there)], f_s.at[h, there], b_r.at[h, there], partner, col
        )

    for h in range(parts):
        for step in range(1, n_col):
            a_copy(h, col_peer(step), col_peer(step)).wait_recv()
        for step in range(2, n_row, 2):
            b_copy(h, row_peer(step), row).start()
        b_copy(h, partner, row).start()

    for step in range(1, n_row):
        id_copy(row_peer(step), row_peer(step)).wait_recv()
    load_anc.wait()

    for side in range(2):
        @pl.loop(0, half)
        def _(q):
            mask_ids = ids[2 * q + side, 0:1, 0:block_height]
            total = jnp.zeros((tile_rows, block_height), F32)
            for b in range(panel_blocks):
                keep = jnp.where(mask_ids == b, 1.0, 0.0)
                total = total + anc[:, b * block_height:(b + 1) * block_height] * keep
            lanes = pl.ds(pl.multiple_of(q * block_height, block_height), block_height)
            perm[side, :, lanes] = total.astype(BF16)

    def block_of(h, m, count=1):
        held = blocks[h, pl.ds(m, count)]
        if height % 16 == 0:
            return held.reshape(count * block_height, part_width)
        return held.astype(F32).reshape(count * block_height, part_width).astype(BF16)

    def half_product(h, side):
        return dot(perm[side], block_of(h, side * half, half))

    root = row * n_col // n_row
    first = (row * tile_rows - root * panel_rows) // block_height

    def c_copy(h, peer, there):
        return copy(
            part.at[h, peer], part_in.at[h, there], c_s.at[h, peer], c_r.at[h, there], row, peer
        )

    def w_copy(h, peer):
        return copy(spread.at[h, peer], own_rows.at[h], w_s.at[h, peer], w_r.at[h], lax.rem(row + (n_row // 2) * (h % 2), n_row), peer)

    def send_sums(h):
        for p in range(n_col):
            part[h, p] = acc[h, p * share:(p + 1) * share, :].astype(BF16)
        for step in range(1, n_col):
            c_copy(h, col_peer(n_col - step), col).start()

    def send_rows(h):
        away = n_row // 2 if h % 2 == 1 else 0
        target = lax.rem(row + away, n_row)
        goal = target * n_col // n_row
        begin = (target * tile_rows - goal * panel_rows) // block_height

        @pl.when(col == root)
        def _():
            if away:
                build(h, row, root, first, False)

        @pl.when(col == goal)
        def _():
            build(h, target, goal, begin, True)

    def build(h, target, goal, begin, send):
        rows = []
        for i in range(tile_rows // block_height):
            chosen = jnp.zeros((block_height, part_width), F32)
            for m in range(n_row):
                keep = jnp.where(ids[m, 0:1, 0:part_width] == begin + i, 1.0, 0.0)
                chosen = chosen + block_of(h, (m % 2) * half + m // 2).astype(F32) * keep
            rows.append(chosen)
        rows = jnp.concatenate(rows, axis=0)
        if not send:
            spare[...] = rows
            own_rows[h] = spare[pl.ds(pl.multiple_of(col * share, 8), share), :].astype(BF16)
            return
        for p in range(n_col):
            spread[h, p] = rows[p * share:(p + 1) * share].astype(BF16)
        for step in range(1, n_col):
            w_copy(h, col_peer(step)).start()
        if h % 2 == 0:
            own_rows[h] = spread[h, col]

    for h in range(parts):
        for step in range(2, n_row, 2):
            m = row_peer(n_row - step)
            b_copy(h, m, m).wait_recv()
            b_forward(h, m).start()
        acc[h] = half_product(h, lax.rem(row, 2))
        for step in range(0, n_row, 2):
            m = lax.rem(partner + n_row - step, n_row)
            b_copy(h, m, m).wait_recv()
        acc[h] += half_product(h, lax.rem(partner, 2))
        if h < parts - 1:
            send_sums(h)
            send_rows(h)
        else:
            send_rows(h)
            send_sums(h)

    f_high, f_low = split(factor[...])
    gram[...] = tdot(f_high, f_high) + tdot(f_high, f_low) + tdot(f_low, f_high)
    width_out = diag.shape[0]
    fdiag[...] = gram[pl.ds(pl.multiple_of(col * width_out, 8), width_out), :]

    def gr_copy(h, peer, there):
        return copy(
            row_out.at[h, peer], row_in.at[h, there], gr_s.at[h, peer], gr_r.at[h, there], peer, col
        )

    def gc_copy(h, peer, there):
        return copy(
            col_out.at[h, peer], col_in.at[h, there], gc_s.at[h, peer], gc_r.at[h, there], row, peer
        )

    def gg_copy(h, peer, there):
        return copy(
            total_in.at[h, there], total_in.at[h, there], gg_s.at[h, peer], gg_r.at[h, there], peer, col
        )

    for h in range(parts):
        lanes = slice(h * part_width, (h + 1) * part_width)
        total = acc[h, pl.ds(pl.multiple_of(col * share, 8), share), :]
        for step in range(1, n_col):
            m = col_peer(step)
            c_copy(h, m, m).wait_recv()
            total = total + part_in[h, m].astype(F32)
        out[:, lanes] = total
        t_high, t_low = split(total)
        for g in range(parts):
            if h == 0:
                @pl.when(col != root)
                def _():
                    w_copy(g, root).wait_recv()
            mine = own_rows[g]
            rows_g = slice(g * part_width, (g + 1) * part_width)
            gram[rows_g, lanes] = tdot(mine, t_high) + tdot(mine, t_low)
        for j in range(n_row):
            for p in range(n_col):
                start = (p * n_row + j) * piece
                row_out[h, j, p] = gram[start:start + piece, lanes].astype(row_out.dtype)
        for step in range(1, n_row):
            gr_copy(h, row_peer(step), row).start()

    for h in range(parts):
        summed = row_out[h, row].astype(F32)
        for step in range(1, n_row):
            m = row_peer(n_row - step)
            gr_copy(h, m, m).wait_recv()
            summed = summed + row_in[h, m].astype(F32)
        col_out[h] = summed
        for step in range(1, n_col):
            gc_copy(h, col_peer(step), col).start()

    for h in range(parts):
        final = col_out[h, col]
        for step in range(1, n_col):
            m = col_peer(n_col - step)
            gc_copy(h, m, m).wait_recv()
            final = final + col_in[h, m]
        total_in[h, row] = final
        for step in range(1, n_row):
            gg_copy(h, row_peer(step), row).start()

    for h in range(parts):
        for step in range(1, n_row):
            m = row_peer(n_row - step)
            gg_copy(h, m, m).wait_recv()
        gathered = jnp.concatenate([total_in[h, m] for m in range(n_row)], axis=0)
        diag[:, h * part_width:(h + 1) * part_width] = gathered

    for h in range(parts):
        for step in range(1, n_col):
            peer = col_peer(step)
            a_copy(h, peer, col).wait_send()
            c_copy(h, peer, col).wait_send()
            gc_copy(h, peer, col).wait_send()
        for step in range(1, n_row):
            peer = row_peer(step)
            if h == 0:
                id_copy(peer, row).wait_send()
            gr_copy(h, peer, row).wait_send()
            gg_copy(h, peer, row).wait_send()
        for step in range(2, n_row, 2):
            b_copy(h, row_peer(step), row).wait_send()
            b_forward(h, row_peer(n_row - step)).wait_send()
        b_copy(h, partner, row).wait_send()

    @pl.when(col == root)
    def _():
        for h in range(parts):
            for step in range(1, n_col):
                pass
    for h in range(parts):
        goal = lax.rem(row + (n_row // 2) * (h % 2), n_row) * n_col // n_row

        @pl.when(col == goal)
        def _():
            for step in range(1, n_col):
                w_copy(h, col_peer(step)).wait_send()


PARTS = 2


def solution(mesh):
    n_row, n_col = mesh.shape["row"], mesh.shape["col"]

    def body(front_rows, slot_blocks, inv_factor, ancestor_inv):
        _, height, width = front_rows.shape
        tile_rows, panel_rows = ancestor_inv.shape
        block_height = height * n_col
        share = tile_rows // n_col
        diag_width = width // n_col
        piece = diag_width // n_row
        parts, part_width = PARTS, width // PARTS
        wire = BF16 if piece % 16 == 0 else F32
        vmem = pltpu.VMEM

        def dma(*shape):
            return pltpu.SemaphoreType.DMA(shape)

        in_vmem = pl.BlockSpec(memory_space=pltpu.VMEM)
        anywhere = pl.BlockSpec(memory_space=pl.ANY)
        total, gram, factor_gram = pl.pallas_call(
            functools.partial(kernel, n_row, n_col, parts),
            out_shape=(
                pltpu.VMEM((share, width), F32),
                pltpu.VMEM((diag_width, width), F32),
                pltpu.VMEM((diag_width, width), F32),
            ),
            in_specs=[in_vmem, pl.BlockSpec(memory_space=pltpu.SMEM), anywhere, anywhere],
            out_specs=(in_vmem, in_vmem, in_vmem),
            scratch_shapes=[
                vmem((width, width), F32),
                vmem((tile_rows, panel_rows), F32),
                vmem((n_row, 8, max(part_width, block_height)), jnp.int32),
                vmem((parts, n_col, height, part_width), BF16),
                vmem((parts, n_row, n_col, height, part_width), BF16),
                vmem((2, tile_rows, n_row // 2 * block_height), BF16),
                vmem((parts, tile_rows, part_width), F32),
                vmem((parts, n_col, share, part_width), BF16),
                vmem((parts, n_col, share, part_width), BF16),
                vmem((parts, share, part_width), BF16),
                vmem((parts, n_col, share, part_width), BF16),
                vmem((tile_rows, part_width), F32),
                vmem((width, width), F32),
                vmem((parts, n_row, n_col, piece, part_width), wire),
                vmem((parts, n_row, n_col, piece, part_width), wire),
                vmem((parts, n_col, piece, part_width), F32),
                vmem((parts, n_col, piece, part_width), F32),
                vmem((parts, n_row, piece, part_width), F32),
                dma(2),
                dma(n_row), dma(n_row),
                dma(parts, n_col), dma(parts, n_col),
                dma(parts, n_row), dma(parts, n_row), dma(parts, n_row),
                dma(parts, n_col), dma(parts, n_col),
                dma(parts, n_col), dma(parts),
                dma(parts, n_row), dma(parts, n_row),
                dma(parts, n_col), dma(parts, n_col),
                dma(parts, n_row), dma(parts, n_row),
            ],
            compiler_params=pltpu.CompilerParams(
                collective_id=0, has_side_effects=True, vmem_limit_bytes=60 * 1024 * 1024
            ),
        )(front_rows, slot_blocks, inv_factor, ancestor_inv)
        return -total, factor_gram + gram

    in_specs = (P("row", "col", None), P("row"), P(), P("row", "col"))
    out_specs = (P(("row", "col"), None), P("col", None))
    return jax.shard_map(body, mesh=mesh, in_specs=in_specs, out_specs=out_specs, check_vma=False)
```
